32 devices in a mesh: mem: 4 (over x, core), lat: 8 (over z, y).
Axes of the slice: x: 2, y: 2, z: 4, core: 2. Of those that a mesh axis runs over, the one named last changes fastest.
Arguments:
- control: float32 [128, 16, 1024], P('mem', 'lat'), may hold values from -6 to 6
- ensemble: float32 [128, 4, 16, 1024], P('mem', None, 'lat'), may hold values from -0.72 to 0.72
- widths: int32 [16], P('lat'), may hold values from 0 to 4
- interp_source: int32 [4, 32, 2048], P(None, 'lat'), may hold values from 0 to 4095, as said below
- interp_weight: float32 [4, 32, 2048], P(None, 'lat'), may hold values from 0.1 to 0.5
- obs_mask: int32 [4, 32, 2048], P(None, 'lat'), may hold values 0 or 1
- innovation: float32 [4, 32, 2048], P(None, 'lat'), may hold values from -12 to 12
Outputs:
- control_next: float32 [128, 16, 1024], P('mem', 'lat')
The draws below stay inside these ranges and needn't reach their ends.
Inputs may be any that keep to these rules, and one draw needn't show every extreme that they name: `interp_source`: for a fine point (j, i) in band b = j // 4 each value is (row - b * 2 + 1) * 1024 + column of a coarse cell inside the grid whose row differs from j // 2 by at most 1 and whose column differs from i // 2 by at most 2, cyclically modulo 1024.
All inputs are finite; a program needn't handle non-finite values. No bound on the sum of `obs_mask` on one device may be relied on, other than what follows from the above.
Results may differ from the reference program's by a relative error of at most 0.0001.
Values sent between devices are 32-bit elements; how exact they have to be, the bound alone decides.
A program may use at most 128 MiB of HBM per device.

```python
import jax
import jax.numpy as jnp
from jax import lax

CLAT = 2
NLON = 1024
NT = 4
WIDEST = 4
GRAD_STEPS = 2
MEMBERS = 128
NLAT = 16
FLON = 2048
NFLAT = 32


def draw_interp_source(key, part):
    key_rows, key_cols = jax.random.split(jax.random.fold_in(key, 7), 2)
    fine_rows = jnp.arange(NFLAT, dtype=jnp.int32)
    band_first = fine_rows // (2 * CLAT) * CLAT
    base_row = fine_rows // 2
    jitter = jax.random.randint(key_rows, (4, NFLAT, FLON), -1, 2)
    coarse_row = base_row[None, :, None] + jitter
    lowest = jnp.maximum(band_first - 1, 0)[None, :, None]
    highest = jnp.minimum(band_first + CLAT, NLAT - 1)[None, :, None]
    coarse_row = jnp.clip(coarse_row, lowest, highest)
    base_col = jnp.arange(FLON, dtype=jnp.int32) // 2
    coarse_col = (base_col[None, None, :] + jax.random.randint(key_cols, (4, NFLAT, FLON), -2, 3)) % NLON
    return ((coarse_row - band_first[None, :, None] + 1) * NLON + coarse_col).astype(jnp.int32)


def set_ends(values, stream_key, least, high):
    longest = values.shape.index(max(values.shape))
    spots = []
    for shift in (0, 1):
        where = [jax.random.randint(jax.random.fold_in(stream_key, axis), (), 0, length) for axis, length in enumerate(values.shape)]
        where[longest] = (where[longest] + shift) % values.shape[longest]
        spots.append(tuple(where))
    return values.at[spots[0]].set(least).at[spots[1]].set(high)


def block_scale(rng, extent, cuts, low, largest):
    loudness, own = 1.0, jax.random.fold_in(rng, 6)
    for dim, parts in cuts:
        heights = jnp.exp(jax.random.uniform(jax.random.fold_in(own, dim), (parts,), jnp.float32, low / len(cuts), largest / len(cuts)))
        loudness = loudness * jnp.repeat(heights, extent[dim] // parts).reshape([-1 if axis == dim else 1 for axis in range(len(extent))])
    return loudness


def scatter_about(stream_key, shape, deviation, limit, cuts=(), kind=jnp.bfloat16):
    loudness = block_scale(stream_key, shape, cuts, -0.22, 0.18) if cuts else 1.0
    result = jax.random.normal(stream_key, shape, jnp.float32) * deviation * loudness
    return jnp.minimum(jnp.maximum(result, -limit), limit).astype(kind)


def setup_inputs(seed: int = 0) -> dict:
    splits = jax.random.split(jax.random.key(seed), 8)
    return {
        "control": scatter_about(splits[0], (MEMBERS, NLAT, NLON), 1.0, 6.0, ((0, 4), (1, 8)), jnp.float32),
        "ensemble": scatter_about(splits[1], (MEMBERS, NT, NLAT, NLON), 0.12, 0.72, ((0, 4), (2, 8)), jnp.float32),
        "widths": set_ends(jax.random.randint(splits[2], (NLAT,), 0, WIDEST + 1), jax.random.fold_in(splits[2], 1), 0, WIDEST).astype(jnp.int32),
        "interp_source": draw_interp_source(jax.random.fold_in(splits[7], 71), 0),
        "interp_weight": jnp.clip(0.1 + 0.4 * jax.random.uniform(splits[4], (4, NFLAT, FLON), jnp.float32) ** block_scale(splits[4], (4, NFLAT, FLON), ((1, 8),), -0.2, 0.2), 0.1, 0.5),
        "obs_mask": set_ends((jax.random.randint(splits[5], (NT, NFLAT, FLON), 0, 2) < 1).astype(jnp.int32), jax.random.fold_in(splits[5], 1), 0, 1),
        "innovation": scatter_about(splits[6], (NT, NFLAT, FLON), 2.0, 12.0, ((1, 8),), jnp.float32),
    }


C_MID = 0.5
C_SIDE = 0.25
STEP_SIZE = 0.5
HIGHEST_PRECISION = lax.Precision.HIGHEST


def lon_filter(source_field, widths):
    scaled = 1.0 / (2.0 * widths.astype(jnp.float32) + 1.0)
    summed = jnp.zeros_like(source_field)
    for offset in range(-WIDEST, WIDEST + 1):
        weight_row = jnp.where(abs(offset) <= widths, scaled, 0.0 * scaled)
        summed = summed + jnp.roll(source_field, offset, axis=-1) * weight_row[:, None]
    return summed


def lat_filter(source_field):
    padded = jnp.pad(source_field, ((0, 0), (1, 1), (0, 0)))
    return C_MID * source_field + C_SIDE * (padded[:, :-2] + padded[:, 2:])


def obs_stencil(fine_field):
    return 0.25 * jnp.roll(fine_field, 1, axis=-1) + 0.5 * fine_field + 0.25 * jnp.roll(fine_field, -1, axis=-1)


def reference(control, ensemble, widths, interp_source, interp_weight, obs_mask, innovation):
    band_index = jnp.arange(NFLAT, dtype=jnp.int32) // (2 * CLAT)
    band_offset = (band_index * (CLAT * NLON)).astype(jnp.int32)[None, :, None]
    flat_source = (interp_source + band_offset).astype(jnp.int32).reshape(-1)
    obs_weight = obs_mask.astype(jnp.float32)
    control_now = control
    for iteration in range(GRAD_STEPS):
        forward = lat_filter(lon_filter(control_now, widths))
        coarse = jnp.einsum("mtri,mri->tri", ensemble, forward, precision=HIGHEST_PRECISION)
        padded = jnp.pad(coarse, ((0, 0), (1, 1), (0, 0))).reshape(NT, -1)
        picked = jnp.take(padded, flat_source, axis=1).reshape((NT,) + interp_weight.shape)
        fine_field = jnp.sum(picked * interp_weight[None], axis=1)
        misfit = obs_weight * (obs_stencil(fine_field) - innovation)
        fine_grid_return = obs_stencil(misfit)
        spread = (fine_grid_return[:, None] * interp_weight[None]).reshape(NT, -1)
        landed = jnp.zeros((NT, (NLAT + 2) * NLON), jnp.float32).at[:, flat_source].add(spread)
        coarse_back = landed.reshape(NT, NLAT + 2, NLON)[:, 1:-1]
        member_back = jnp.einsum("mtri,tri->mri", ensemble, coarse_back, precision=HIGHEST_PRECISION)
        gradient = control_now + lon_filter(lat_filter(member_back), widths)
        control_now = control_now - STEP_SIZE * gradient
    return control_now
```

```python
import functools

import jax
import jax.numpy as jnp
from jax import lax
from jax.experimental import pallas as pl
from jax.experimental.pallas import tpu as pltpu
from jax.sharding import PartitionSpec as P

WIDEST = 4
GRAD_STEPS = 2
C_MID = 0.5
C_SIDE = 0.25
STEP_SIZE = 0.5
GROUP = 8
LANES = 128
REACH = 2
COLS = 2 * REACH + 1
MESH = pl.DeviceIdType.MESH


def rolled(x, shift):
    shift = shift % x.shape[-1]
    return x if shift == 0 else pltpu.roll(x, shift, x.ndim - 1)


def lon_filter(x, weights):
    total = x * weights[0]
    for k in range(1, WIDEST + 1):
        total = total + (rolled(x, k) + rolled(x, -k)) * weights[k]
    return total


def stencil(even, odd):
    return (
        0.25 * (rolled(odd, 1) + odd) + 0.5 * even,
        0.25 * (even + rolled(even, -1)) + 0.5 * odd,
    )


def kernel(
    sizes,
    widths,
    control,
    ensemble,
    source,
    weight,
    obs_mask,
    innovation,
    out,
    ens,
    now,
    edge,
    halo,
    forward,
    result,
    rows_in,
    rows_out,
    planes,
    mask,
    target,
    fine,
    part,
    peers,
    coarse,
    rim,
    land,
    land_rim,
    back,
    load_sem,
    edge_send,
    edge_recv,
    peer_send,
    peer_recv,
    rim_send,
    rim_recv,
    land_send,
    land_recv,
):
    slots, members, rows, lon, mem_count, lat_count = sizes
    groups = members // GROUP
    me_mem = lax.axis_index("mem")
    me_lat = lax.axis_index("lat")
    has = (me_lat > 0, me_lat < lat_count - 1)
    beside = (me_lat - 1, me_lat + 1)

    loads = []
    for r in range(rows):
        loads.append(pltpu.make_async_copy(control.at[:, r, :], now.at[r], load_sem.at[r]))
        loads[-1].start()
    for t in range(slots):
        for r in range(rows):
            number = rows + t * rows + r
            loads.append(
                pltpu.make_async_copy(ensemble.at[:, t, r, :], ens.at[t, r], load_sem.at[number])
            )
            loads[-1].start()

    barrier = pltpu.get_barrier_semaphore()
    for d in range(1, mem_count):
        pl.semaphore_signal(
            barrier,
            inc=1,
            device_id={"mem": lax.rem(me_mem + d, mem_count)},
            device_id_type=MESH,
        )
    for side in range(2):

        @pl.when(has[side])
        def _():
            pl.semaphore_signal(
                barrier, inc=1, device_id={"lat": beside[side]}, device_id_type=MESH
            )

    pl.semaphore_wait(
        barrier, mem_count - 1 + has[0].astype(jnp.int32) + has[1].astype(jnp.int32)
    )

    def to_side(side, src, dst, send, recv):
        return pltpu.make_async_remote_copy(
            src_ref=src,
            dst_ref=dst,
            send_sem=send,
            recv_sem=recv,
            device_id={"lat": beside[side]},
            device_id_type=MESH,
        )

    def edge_copy(phase, side, g):
        row = 0 if side == 0 else rows - 1
        part_of = pl.ds(g * GROUP, GROUP)
        return to_side(
            side,
            edge.at[phase, row, part_of],
            halo.at[phase, 1 - side, part_of],
            edge_send.at[phase, side, g],
            edge_recv.at[phase, 1 - side, g],
        )

    def edge_start(phase, g):
        for side in range(2):

            @pl.when(has[side])
            def _():
                edge_copy(phase, side, g).start()

    def edge_wait(phase, g):
        for side in range(2):

            @pl.when(has[side])
            def _():
                edge_copy(phase, 1 - side, g).wait_recv()

    def edge_done(phase):
        for g in range(groups):
            for side in range(2):

                @pl.when(has[side])
                def _():
                    edge_copy(phase, side, g).wait_send()

    weights = []
    for r in range(rows):
        width = widths[r]
        scale = jnp.float32(1.0 / (2 * WIDEST + 1))
        for w in range(WIDEST):
            scale = jnp.where(width == w, jnp.float32(1.0 / (2 * w + 1)), scale)
        weights.append(
            [jnp.where(width >= k, scale, jnp.float32(0.0)) for k in range(WIDEST + 1)]
        )

    def spread(phase, g):
        part_of = pl.ds(g * GROUP, GROUP)
        own = [edge[phase, r, part_of, :] for r in range(rows)]
        padded = [halo[phase, 0, part_of, :], *own, halo[phase, 1, part_of, :]]
        return [
            C_MID * padded[r + 1] + C_SIDE * (padded[r] + padded[r + 2]) for r in range(rows)
        ]

    for side in range(2):

        @pl.when(jnp.logical_not(has[side]))
        def _():
            for phase in range(2 * GRAD_STEPS):
                halo[phase, side] = jnp.zeros((members, lon), jnp.float32)
            for step in range(GRAD_STEPS):
                rim[step, side] = jnp.zeros((slots, lon), jnp.float32)
                land_rim[step, side] = jnp.zeros((slots, lon), jnp.float32)

    for r in range(rows):
        loads[r].wait()
    for g in range(groups):
        part_of = pl.ds(g * GROUP, GROUP)
        for r in range(rows):
            edge[0, r, part_of, :] = lon_filter(now[r, part_of, :], weights[r])
        edge_start(0, g)

    fine_rows = 2 * rows
    four = source.shape[0]
    for s in range(four):
        rows_in[pl.ds(s * fine_rows, fine_rows), :] = source[s].astype(jnp.float32)
        rows_in[pl.ds((four + s) * fine_rows, fine_rows), :] = weight[s]
    for r in range(rows):
        for jj in range(2):
            top = 2 * four * fine_rows + (r * 2 + jj) * slots
            rows_in[pl.ds(top, slots), :] = obs_mask[:, 2 * r + jj, :].astype(jnp.float32)
            top = top + rows * 2 * slots
            rows_in[pl.ds(top, slots), :] = innovation[:, 2 * r + jj, :]
    line = lax.broadcasted_iota(jnp.int32, (2 * LANES, 2 * LANES), 0)
    column = lax.broadcasted_iota(jnp.int32, (2 * LANES, 2 * LANES), 1)
    wanted = jnp.where(column < LANES, 2 * column, 2 * (column - LANES) + 1)
    pick = jnp.where(line == wanted, 1.0, 0.0).astype(jnp.float32)
    for block in range(lon // LANES):
        both = jnp.dot(
            rows_in[:, pl.ds(block * 2 * LANES, 2 * LANES)],
            pick,
            precision=lax.Precision.HIGHEST,
            preferred_element_type=jnp.float32,
        )
        rows_out[0, :, pl.ds(block * LANES, LANES)] = both[:, :LANES]
        rows_out[1, :, pl.ds(block * LANES, LANES)] = both[:, LANES:]
    across = lax.broadcasted_iota(jnp.int32, (2 * slots, lon), 1).astype(jnp.float32)
    for r in range(rows):
        for p in range(2):
            top = 2 * four * fine_rows + r * 2 * slots
            mask[r, p] = rows_out[p, pl.ds(top, 2 * slots), :]
            target[r, p] = rows_out[p, pl.ds(top + rows * 2 * slots, 2 * slots), :]
            codes, heavy = [], []
            for s in range(four):
                pair_code, pair_weight = [], []
                for jj in range(2):
                    at = s * fine_rows + 2 * r + jj
                    pair_code.append(
                        jnp.broadcast_to(rows_out[p, pl.ds(at, 1), :], (slots, lon))
                    )
                    at = at + four * fine_rows
                    pair_weight.append(
                        jnp.broadcast_to(rows_out[p, pl.ds(at, 1), :], (slots, lon))
                    )
                flat = jnp.floor(jnp.concatenate(pair_code, axis=0) + 0.5)
                line_of = jnp.floor((flat + 0.5) * (1.0 / lon))
                shift = flat - line_of * lon - across + REACH
                shift = jnp.where(shift < 0.0, shift + lon, shift)
                shift = jnp.where(shift >= lon, shift - lon, shift)
                codes.append((line_of - r) * COLS + shift)
                heavy.append(jnp.concatenate(pair_weight, axis=0))
            for number in range(3 * COLS):
                total = jnp.where(codes[0] == number, heavy[0], 0.0)
                for s in range(1, four):
                    total = total + jnp.where(codes[s] == number, heavy[s], 0.0)
                planes[number, r, p] = total

    for load in loads[rows:]:
        load.wait()

    for step in range(GRAD_STEPS):
        for g in range(groups):
            edge_wait(2 * step, g)
            spreads = spread(2 * step, g)
            for r in range(rows):
                forward[r, pl.ds(g * GROUP, GROUP), :] = spreads[r]
        for r in range(rows):
            for t in range(slots):
                total = jnp.zeros((GROUP, lon), jnp.float32)
                for g in range(groups):
                    part_of = pl.ds(g * GROUP, GROUP)
                    total = total + ens[t, r, part_of, :] * forward[r, part_of, :]
                part[step, r, pl.ds(t, 1), :] = jnp.sum(total, axis=0, keepdims=True)

        copies = []
        for d in range(1, mem_count):
            copies.append(
                pltpu.make_async_remote_copy(
                    src_ref=part.at[step],
                    dst_ref=peers.at[step, d - 1],
                    send_sem=peer_send.at[step, d - 1],
                    recv_sem=peer_recv.at[step, d - 1],
                    device_id={"mem": lax.rem(me_mem + d, mem_count)},
                    device_id_type=MESH,
                )
            )
            copies[-1].start()
        for copy in copies:
            copy.wait_recv()
        for r in range(rows):
            total = part[step, r]
            for d in range(1, mem_count):
                total = total + peers[step, d - 1, r]
            coarse[step, r] = total

        def rim_copy(side):
            return to_side(
                side,
                coarse.at[step, 0 if side == 0 else rows - 1],
                rim.at[step, 1 - side],
                rim_send.at[step, side],
                rim_recv.at[step, 1 - side],
            )

        for side in range(2):

            @pl.when(has[side])
            def _():
                rim_copy(side).start()

        def interpolate(line_of, values, first):
            doubled = jnp.concatenate([values, values], axis=0)
            moved = [rolled(doubled, -shift) for shift in range(-REACH, REACH + 1)]
            for r in range(rows):
                if abs(line_of - r) > 1:
                    continue
                for p in range(2):
                    total = None
                    for col in range(COLS):
                        term = planes[(line_of - r + 1) * COLS + col, r, p] * moved[col]
                        total = term if total is None else total + term
                    if r in first:
                        fine[r, p] = fine[r, p] + total
                    else:
                        fine[r, p] = total
                first.add(r)

        first = set()
        for r in range(rows):
            interpolate(r, coarse[step, r], first)
        for side in range(2):

            @pl.when(has[side])
            def _():
                rim_copy(1 - side).wait_recv()

        interpolate(-1, rim[step, 0], first)
        interpolate(rows, rim[step, 1], first)

        backs = []
        for r in range(rows):
            even, odd = stencil(fine[r, 0], fine[r, 1])
            even = mask[r, 0] * (even - target[r, 0])
            odd = mask[r, 1] * (odd - target[r, 1])
            backs.append(stencil(even, odd))
        for line_of in range(-1, rows + 1):
            landed = None
            for col in range(COLS):
                gathered = None
                for r in range(rows):
                    if abs(line_of - r) > 1:
                        continue
                    for p in range(2):
                        term = planes[(line_of - r + 1) * COLS + col, r, p] * backs[r][p]
                        gathered = term if gathered is None else gathered + term
                gathered = rolled(gathered, col - REACH)
                landed = gathered if landed is None else landed + gathered
            land[step, line_of + 1] = landed[:slots] + landed[slots:]

        def land_copy(side):
            return to_side(
                side,
                land.at[step, 0 if side == 0 else rows + 1],
                land_rim.at[step, 1 - side],
                land_send.at[step, side],
                land_recv.at[step, 1 - side],
            )

        for side in range(2):

            @pl.when(has[side])
            def _():
                land_copy(side).start()

        for side in range(2):

            @pl.when(has[side])
            def _():
                land_copy(1 - side).wait_recv()

        for r in range(rows):
            total = land[step, r + 1]
            if r == 0:
                total = total + land_rim[step, 0]
            if r == rows - 1:
                total = total + land_rim[step, 1]
            back[r] = total

        for g in range(groups):
            part_of = pl.ds(g * GROUP, GROUP)
            for r in range(rows):
                total = None
                for t in range(slots):
                    term = ens[t, r, part_of, :] * back[r, pl.ds(t, 1), :]
                    total = term if total is None else total + term
                edge[2 * step + 1, r, part_of, :] = total
            edge_start(2 * step + 1, g)
        for g in range(groups):
            part_of = pl.ds(g * GROUP, GROUP)
            edge_wait(2 * step + 1, g)
            spreads = spread(2 * step + 1, g)
            for r in range(rows):
                before = now[r, part_of, :]
                after = before - STEP_SIZE * (before + lon_filter(spreads[r], weights[r]))
                if step < GRAD_STEPS - 1:
                    now[r, part_of, :] = after
                    edge[2 * step + 2, r, part_of, :] = lon_filter(after, weights[r])
                else:
                    result[r, part_of, :] = after
            if step < GRAD_STEPS - 1:
                edge_start(2 * step + 2, g)

        for copy in copies:
            copy.wait_send()
        for side in range(2):

            @pl.when(has[side])
            def _():
                rim_copy(side).wait_send()
                land_copy(side).wait_send()

    stores = []
    for r in range(rows):
        stores.append(pltpu.make_async_copy(result.at[r], out.at[:, r, :], load_sem.at[r]))
        stores[-1].start()
    for phase in range(2 * GRAD_STEPS):
        edge_done(phase)
    for store in stores:
        store.wait()


def local(control, ensemble, widths, source, weight, obs_mask, innovation):
    members, slots, rows, lon = ensemble.shape
    mem_count, lat_count = lax.axis_size("mem"), lax.axis_size("lat")
    phases = 2 * GRAD_STEPS
    fine_rows = 2 * rows
    f32 = jnp.float32
    vmem = pl.BlockSpec(memory_space=pltpu.VMEM)
    anywhere = pl.BlockSpec(memory_space=pl.ANY)
    groups = members // GROUP
    stacked = 2 * source.shape[0] * fine_rows + 2 * slots * fine_rows
    dma = pltpu.SemaphoreType.DMA
    return pl.pallas_call(
        functools.partial(kernel, (slots, members, rows, lon, mem_count, lat_count)),
        out_shape=jax.ShapeDtypeStruct(control.shape, f32),
        in_specs=[
            pl.BlockSpec(memory_space=pltpu.SMEM),
            anywhere,
            anywhere,
            vmem,
            vmem,
            vmem,
            vmem,
        ],
        out_specs=anywhere,
        scratch_shapes=[
            pltpu.VMEM((slots, rows, members, lon), f32),
            pltpu.VMEM((rows, members, lon), f32),
            pltpu.VMEM((phases, rows, members, lon), f32),
            pltpu.VMEM((phases, 2, members, lon), f32),
            pltpu.VMEM((rows, members, lon), f32),
            pltpu.VMEM((rows, members, lon), f32),
            pltpu.VMEM((stacked, 2 * lon), f32),
            pltpu.VMEM((2, stacked, lon), f32),
            pltpu.VMEM((3 * COLS, rows, 2, 2 * slots, lon), f32),
            pltpu.VMEM((rows, 2, 2 * slots, lon), f32),
            pltpu.VMEM((rows, 2, 2 * slots, lon), f32),
            pltpu.VMEM((rows, 2, 2 * slots, lon), f32),
            pltpu.VMEM((GRAD_STEPS, rows, slots, lon), f32),
            pltpu.VMEM((GRAD_STEPS, mem_count - 1, rows, slots, lon), f32),
            pltpu.VMEM((GRAD_STEPS, rows, slots, lon), f32),
            pltpu.VMEM((GRAD_STEPS, 2, slots, lon), f32),
            pltpu.VMEM((GRAD_STEPS, rows + 2, slots, lon), f32),
            pltpu.VMEM((GRAD_STEPS, 2, slots, lon), f32),
            pltpu.VMEM((rows, slots, lon), f32),
            dma((rows + slots * rows,)),
            dma((phases, 2, groups)),
            dma((phases, 2, groups)),
            dma((GRAD_STEPS, mem_count - 1)),
            dma((GRAD_STEPS, mem_count - 1)),
            dma((GRAD_STEPS, 2)),
            dma((GRAD_STEPS, 2)),
            dma((GRAD_STEPS, 2)),
            dma((GRAD_STEPS, 2)),
        ],
        compiler_params=pltpu.CompilerParams(
            collective_id=0, has_side_effects=True, vmem_limit_bytes=48 * 1024 * 1024
        ),
    )(widths, control, ensemble, source, weight, obs_mask, innovation)


def solution(mesh):
    in_specs = (
        P("mem", "lat", None),
        P("mem", None, "lat", None),
        P("lat"),
        P(None, "lat", None),
        P(None, "lat", None),
        P(None, "lat", None),
        P(None, "lat", None),
    )
    out_specs = P("mem", "lat", None)
    return jax.shard_map(local, mesh=mesh, in_specs=in_specs, out_specs=out_specs, check_vma=False)
```

```python
import functools

import jax
import jax.numpy as jnp
from jax import lax
from jax.experimental import pallas as pl
from jax.experimental.pallas import tpu as pltpu
from jax.sharding import PartitionSpec as P

WIDEST = 4
GRAD_STEPS = 2
C_MID = 0.5
C_SIDE = 0.25
STEP_SIZE = 0.5
GROUP = 8
LANES = 128
REACH = 2
COLS = 2 * REACH + 1
MESH = pl.DeviceIdType.MESH


def rolled(x, shift):
    shift = shift % x.shape[-1]
    return x if shift == 0 else pltpu.roll(x, shift, x.ndim - 1)


def lon_filter(x, weights):
    total = x * weights[0]
    for k in range(1, WIDEST + 1):
        total = total + (rolled(x, k) + rolled(x, -k)) * weights[k]
    return total


def stencil(even, odd):
    return (
        0.25 * (rolled(odd, 1) + odd) + 0.5 * even,
        0.25 * (even + rolled(even, -1)) + 0.5 * odd,
    )


def kernel(
    sizes,
    widths_far,
    control,
    ensemble,
    source_far,
    weight_far,
    obs_mask_far,
    innovation_far,
    out,
    widths,
    source,
    weight,
    obs_mask,
    innovation,
    ens,
    now,
    edge,
    halo,
    forward,
    result,
    rows_in,
    rows_out,
    planes,
    mask,
    target,
    fine,
    part,
    peers,
    coarse,
    rim,
    land,
    land_rim,
    back,
    load_sem,
    store_sem,
    edge_send,
    edge_recv,
    peer_send,
    peer_recv,
    rim_send,
    rim_recv,
    land_send,
    land_recv,
):
    slots, members, rows, lon, mem_count, lat_count = sizes
    groups = members // GROUP
    me_mem = lax.axis_index("mem")
    me_lat = lax.axis_index("lat")
    has = (me_lat > 0, me_lat < lat_count - 1)
    beside = (me_lat - 1, me_lat + 1)

    loads = []

    def load(src, dst):
        loads.append(pltpu.make_async_copy(src, dst, load_sem.at[len(loads)]))
        loads[-1].start()

    load(widths_far, widths)
    for r in range(rows):
        load(control.at[:, r, :], now.at[r])
    load(source_far, source)
    load(weight_far, weight)
    load(obs_mask_far, obs_mask)
    load(innovation_far, innovation)
    for t in range(slots):
        for r in range(rows):
            load(ensemble.at[:, t, r, :], ens.at[t, r])

    barrier = pltpu.get_barrier_semaphore()
    for d in range(1, mem_count):
        pl.semaphore_signal(
            barrier,
            inc=1,
            device_id={"mem": lax.rem(me_mem + d, mem_count)},
            device_id_type=MESH,
        )
    for side in range(2):

        @pl.when(has[side])
        def _():
            pl.semaphore_signal(
                barrier, inc=1, device_id={"lat": beside[side]}, device_id_type=MESH
            )

    pl.semaphore_wait(
        barrier, mem_count - 1 + has[0].astype(jnp.int32) + has[1].astype(jnp.int32)
    )

    def to_side(side, src, dst, send, recv):
        return pltpu.make_async_remote_copy(
            src_ref=src,
            dst_ref=dst,
            send_sem=send,
            recv_sem=recv,
            device_id={"lat": beside[side]},
            device_id_type=MESH,
        )

    def edge_copy(phase, side, g):
        row = 0 if side == 0 else rows - 1
        part_of = pl.ds(g * GROUP, GROUP)
        return to_side(
            side,
            edge.at[phase, row, part_of],
            halo.at[phase, 1 - side, part_of],
            edge_send.at[phase, side, g],
            edge_recv.at[phase, 1 - side, g],
        )

    def edge_start(phase, g):
        for side in range(2):

            @pl.when(has[side])
            def _():
                edge_copy(phase, side, g).start()

    def edge_wait(phase, g):
        for side in range(2):

            @pl.when(has[side])
            def _():
                edge_copy(phase, 1 - side, g).wait_recv()

    def edge_done(phase):
        for g in range(groups):
            for side in range(2):

                @pl.when(has[side])
                def _():
                    edge_copy(phase, side, g).wait_send()

    loads[0].wait()
    weights = []
    for r in range(rows):
        width = widths[r]
        scale = jnp.float32(1.0 / (2 * WIDEST + 1))
        for w in range(WIDEST):
            scale = jnp.where(width == w, jnp.float32(1.0 / (2 * w + 1)), scale)
        weights.append(
            [jnp.where(width >= k, scale, jnp.float32(0.0)) for k in range(WIDEST + 1)]
        )

    def spread(phase, g):
        part_of = pl.ds(g * GROUP, GROUP)
        own = [edge[phase, r, part_of, :] for r in range(rows)]
        padded = [halo[phase, 0, part_of, :], *own, halo[phase, 1, part_of, :]]
        return [
            C_MID * padded[r + 1] + C_SIDE * (padded[r] + padded[r + 2]) for r in range(rows)
        ]

    for side in range(2):

        @pl.when(jnp.logical_not(has[side]))
        def _():
            for phase in range(2 * GRAD_STEPS):
                halo[phase, side] = jnp.zeros((members, lon), jnp.float32)
            for step in range(GRAD_STEPS):
                rim[step, side] = jnp.zeros((slots, lon), jnp.float32)
                land_rim[step, side] = jnp.zeros((slots, lon), jnp.float32)

    for r in range(rows):
        loads[1 + r].wait()
    for g in range(groups):
        part_of = pl.ds(g * GROUP, GROUP)
        for r in range(rows):
            edge[0, r, part_of, :] = lon_filter(now[r, part_of, :], weights[r])
        edge_start(0, g)

    early = 1 + rows + 4
    for copy in loads[1 + rows : early]:
        copy.wait()
    fine_rows = 2 * rows
    four = source.shape[0]
    for s in range(four):
        rows_in[pl.ds(s * fine_rows, fine_rows), :] = source[s].astype(jnp.float32)
        rows_in[pl.ds((four + s) * fine_rows, fine_rows), :] = weight[s]
    for r in range(rows):
        for jj in range(2):
            top = 2 * four * fine_rows + (r * 2 + jj) * slots
            rows_in[pl.ds(top, slots), :] = obs_mask[:, 2 * r + jj, :].astype(jnp.float32)
            top = top + rows * 2 * slots
            rows_in[pl.ds(top, slots), :] = innovation[:, 2 * r + jj, :]
    line = lax.broadcasted_iota(jnp.int32, (2 * LANES, 2 * LANES), 0)
    column = lax.broadcasted_iota(jnp.int32, (2 * LANES, 2 * LANES), 1)
    wanted = jnp.where(column < LANES, 2 * column, 2 * (column - LANES) + 1)
    pick = jnp.where(line == wanted, 1.0, 0.0).astype(jnp.float32)
    for block in range(lon // LANES):
        both = jnp.dot(
            rows_in[:, pl.ds(block * 2 * LANES, 2 * LANES)],
            pick,
            precision=lax.Precision.HIGHEST,
            preferred_element_type=jnp.float32,
        )
        rows_out[0, :, pl.ds(block * LANES, LANES)] = both[:, :LANES]
        rows_out[1, :, pl.ds(block * LANES, LANES)] = both[:, LANES:]
    across = lax.broadcasted_iota(jnp.int32, (2 * slots, lon), 1).astype(jnp.float32)
    for r in range(rows):
        for p in range(2):
            top = 2 * four * fine_rows + r * 2 * slots
            mask[r, p] = rows_out[p, pl.ds(top, 2 * slots), :]
            target[r, p] = rows_out[p, pl.ds(top + rows * 2 * slots, 2 * slots), :]
            codes, heavy = [], []
            for s in range(four):
                pair_code, pair_weight = [], []
                for jj in range(2):
                    at = s * fine_rows + 2 * r + jj
                    pair_code.append(
                        jnp.broadcast_to(rows_out[p, pl.ds(at, 1), :], (slots, lon))
                    )
                    at = at + four * fine_rows
                    pair_weight.append(
                        jnp.broadcast_to(rows_out[p, pl.ds(at, 1), :], (slots, lon))
                    )
                flat = jnp.floor(jnp.concatenate(pair_code, axis=0) + 0.5)
                line_of = jnp.floor((flat + 0.5) * (1.0 / lon))
                shift = flat - line_of * lon - across + REACH
                shift = jnp.where(shift < 0.0, shift + lon, shift)
                shift = jnp.where(shift >= lon, shift - lon, shift)
                codes.append((line_of - r) * COLS + shift)
                heavy.append(jnp.concatenate(pair_weight, axis=0))
            for number in range(3 * COLS):
                total = jnp.where(codes[0] == number, heavy[0], 0.0)
                for s in range(1, four):
                    total = total + jnp.where(codes[s] == number, heavy[s], 0.0)
                planes[number, r, p] = total

    for copy in loads[early:]:
        copy.wait()

    stores = []
    for step in range(GRAD_STEPS):
        for g in range(groups):
            edge_wait(2 * step, g)
            spreads = spread(2 * step, g)
            for r in range(rows):
                forward[r, pl.ds(g * GROUP, GROUP), :] = spreads[r]
        for r in range(rows):
            for t in range(slots):
                total = jnp.zeros((GROUP, lon), jnp.float32)
                for g in range(groups):
                    part_of = pl.ds(g * GROUP, GROUP)
                    total = total + ens[t, r, part_of, :] * forward[r, part_of, :]
                part[step, r, pl.ds(t, 1), :] = jnp.sum(total, axis=0, keepdims=True)

        copies = []
        for d in range(1, mem_count):
            copies.append(
                pltpu.make_async_remote_copy(
                    src_ref=part.at[step],
                    dst_ref=peers.at[step, d - 1],
                    send_sem=peer_send.at[step, d - 1],
                    recv_sem=peer_recv.at[step, d - 1],
                    device_id={"mem": lax.rem(me_mem + d, mem_count)},
                    device_id_type=MESH,
                )
            )
            copies[-1].start()
        for copy in copies:
            copy.wait_recv()
        for r in range(rows):
            total = part[step, r]
            for d in range(1, mem_count):
                total = total + peers[step, d - 1, r]
            coarse[step, r] = total

        def rim_copy(side):
            return to_side(
                side,
                coarse.at[step, 0 if side == 0 else rows - 1],
                rim.at[step, 1 - side],
                rim_send.at[step, side],
                rim_recv.at[step, 1 - side],
            )

        for side in range(2):

            @pl.when(has[side])
            def _():
                rim_copy(side).start()

        def interpolate(line_of, values, first):
            doubled = jnp.concatenate([values, values], axis=0)
            moved = [rolled(doubled, -shift) for shift in range(-REACH, REACH + 1)]
            for r in range(rows):
                if abs(line_of - r) > 1:
                    continue
                for p in range(2):
                    total = None
                    for col in range(COLS):
                        term = planes[(line_of - r + 1) * COLS + col, r, p] * moved[col]
                        total = term if total is None else total + term
                    if r in first:
                        fine[r, p] = fine[r, p] + total
                    else:
                        fine[r, p] = total
                first.add(r)

        first = set()
        for r in range(rows):
            interpolate(r, coarse[step, r], first)
        for side in range(2):

            @pl.when(has[side])
            def _():
                rim_copy(1 - side).wait_recv()

        interpolate(-1, rim[step, 0], first)
        interpolate(rows, rim[step, 1], first)

        backs = []
        for r in range(rows):
            even, odd = stencil(fine[r, 0], fine[r, 1])
            even = mask[r, 0] * (even - target[r, 0])
            odd = mask[r, 1] * (odd - target[r, 1])
            backs.append(stencil(even, odd))
        for line_of in range(-1, rows + 1):
            landed = None
            for col in range(COLS):
                gathered = None
                for r in range(rows):
                    if abs(line_of - r) > 1:
                        continue
                    for p in range(2):
                        term = planes[(line_of - r + 1) * COLS + col, r, p] * backs[r][p]
                        gathered = term if gathered is None else gathered + term
                gathered = rolled(gathered, col - REACH)
                landed = gathered if landed is None else landed + gathered
            land[step, line_of + 1] = landed[:slots] + landed[slots:]

        def land_copy(side):
            return to_side(
                side,
                land.at[step, 0 if side == 0 else rows + 1],
                land_rim.at[step, 1 - side],
                land_send.at[step, side],
                land_recv.at[step, 1 - side],
            )

        for side in range(2):

            @pl.when(has[side])
            def _():
                land_copy(side).start()

        for side in range(2):

            @pl.when(has[side])
            def _():
                land_copy(1 - side).wait_recv()

        for r in range(rows):
            total = land[step, r + 1]
            if r == 0:
                total = total + land_rim[step, 0]
            if r == rows - 1:
                total = total + land_rim[step, 1]
            back[r] = total

        for g in range(groups):
            part_of = pl.ds(g * GROUP, GROUP)
            for r in range(rows):
                total = None
                for t in range(slots):
                    term = ens[t, r, part_of, :] * back[r, pl.ds(t, 1), :]
                    total = term if total is None else total + term
                edge[2 * step + 1, r, part_of, :] = total
            edge_start(2 * step + 1, g)
        for g in range(groups):
            part_of = pl.ds(g * GROUP, GROUP)
            edge_wait(2 * step + 1, g)
            spreads = spread(2 * step + 1, g)
            for r in range(rows):
                before = now[r, part_of, :]
                after = before - STEP_SIZE * (before + lon_filter(spreads[r], weights[r]))
                if step < GRAD_STEPS - 1:
                    now[r, part_of, :] = after
                    edge[2 * step + 2, r, part_of, :] = lon_filter(after, weights[r])
                else:
                    result[r, part_of, :] = after
                    stores.append(
                        pltpu.make_async_copy(
                            result.at[r, part_of], out.at[part_of, r, :], store_sem.at[r, g]
                        )
                    )
                    stores[-1].start()
            if step < GRAD_STEPS - 1:
                edge_start(2 * step + 2, g)

        for copy in copies:
            copy.wait_send()
        for side in range(2):

            @pl.when(has[side])
            def _():
                rim_copy(side).wait_send()
                land_copy(side).wait_send()

    for phase in range(2 * GRAD_STEPS):
        edge_done(phase)
    for store in stores:
        store.wait()


def local(control, ensemble, widths, source, weight, obs_mask, innovation):
    members, slots, rows, lon = ensemble.shape
    mem_count, lat_count = lax.axis_size("mem"), lax.axis_size("lat")
    phases = 2 * GRAD_STEPS
    fine_rows = 2 * rows
    f32 = jnp.float32
    hbm = pl.BlockSpec(memory_space=pltpu.HBM)
    groups = members // GROUP
    stacked = 2 * source.shape[0] * fine_rows + 2 * slots * fine_rows
    dma = pltpu.SemaphoreType.DMA
    return pl.pallas_call(
        functools.partial(kernel, (slots, members, rows, lon, mem_count, lat_count)),
        out_shape=jax.ShapeDtypeStruct(control.shape, f32),
        in_specs=[hbm] * 7,
        out_specs=hbm,
        scratch_shapes=[
            pltpu.SMEM(widths.shape, jnp.int32),
            pltpu.VMEM(source.shape, jnp.int32),
            pltpu.VMEM(weight.shape, f32),
            pltpu.VMEM(obs_mask.shape, jnp.int32),
            pltpu.VMEM(innovation.shape, f32),
            pltpu.VMEM((slots, rows, members, lon), f32),
            pltpu.VMEM((rows, members, lon), f32),
            pltpu.VMEM((phases, rows, members, lon), f32),
            pltpu.VMEM((phases, 2, members, lon), f32),
            pltpu.VMEM((rows, members, lon), f32),
            pltpu.VMEM((rows, members, lon), f32),
            pltpu.VMEM((stacked, 2 * lon), f32),
            pltpu.VMEM((2, stacked, lon), f32),
            pltpu.VMEM((3 * COLS, rows, 2, 2 * slots, lon), f32),
            pltpu.VMEM((rows, 2, 2 * slots, lon), f32),
            pltpu.VMEM((rows, 2, 2 * slots, lon), f32),
            pltpu.VMEM((rows, 2, 2 * slots, lon), f32),
            pltpu.VMEM((GRAD_STEPS, rows, slots, lon), f32),
            pltpu.VMEM((GRAD_STEPS, mem_count - 1, rows, slots, lon), f32),
            pltpu.VMEM((GRAD_STEPS, rows, slots, lon), f32),
            pltpu.VMEM((GRAD_STEPS, 2, slots, lon), f32),
            pltpu.VMEM((GRAD_STEPS, rows + 2, slots, lon), f32),
            pltpu.VMEM((GRAD_STEPS, 2, slots, lon), f32),
            pltpu.VMEM((rows, slots, lon), f32),
            dma((5 + rows + slots * rows,)),
            dma((rows, groups)),
            dma((phases, 2, groups)),
            dma((phases, 2, groups)),
            dma((GRAD_STEPS, mem_count - 1)),
            dma((GRAD_STEPS, mem_count - 1)),
            dma((GRAD_STEPS, 2)),
            dma((GRAD_STEPS, 2)),
            dma((GRAD_STEPS, 2)),
            dma((GRAD_STEPS, 2)),
        ],
        compiler_params=pltpu.CompilerParams(
            collective_id=0, has_side_effects=True, vmem_limit_bytes=67043328
        ),
    )(widths, control, ensemble, source, weight, obs_mask, innovation)


def solution(mesh):
    in_specs = (
        P("mem", "lat", None),
        P("mem", None, "lat", None),
        P("lat"),
        P(None, "lat", None),
        P(None, "lat", None),
        P(None, "lat", None),
        P(None, "lat", None),
    )
    out_specs = P("mem", "lat", None)
    return jax.shard_map(local, mesh=mesh, in_specs=in_specs, out_specs=out_specs, check_vma=False)
```

```python
import functools

import jax
import jax.numpy as jnp
from jax import lax
from jax.experimental import pallas as pl
from jax.experimental.pallas import tpu as pltpu
from jax.sharding import PartitionSpec as P

WIDEST = 4
GRAD_STEPS = 2
C_MID = 0.5
C_SIDE = 0.25
STEP_SIZE = 0.5
GROUP = 8
LANES = 128
REACH = 2
COLS = 2 * REACH + 1
MESH = pl.DeviceIdType.MESH


def rolled(x, shift):
    shift = shift % x.shape[-1]
    return x if shift == 0 else pltpu.roll(x, shift, x.ndim - 1)


def lon_filter(x, weights):
    total = x * weights[0]
    for k in range(1, WIDEST + 1):
        total = total + (rolled(x, k) + rolled(x, -k)) * weights[k]
    return total


def stencil(even, odd):
    return (
        0.25 * (rolled(odd, 1) + odd) + 0.5 * even,
        0.25 * (even + rolled(even, -1)) + 0.5 * odd,
    )


def kernel(
    sizes,
    widths_far,
    control,
    ensemble,
    source_far,
    weight_far,
    obs_mask_far,
    innovation_far,
    out,
    widths,
    source,
    weight,
    obs_mask,
    innovation,
    ens,
    now,
    edge,
    halo,
    forward,
    result,
    rows_in,
    rows_out,
    planes,
    mask,
    target,
    part,
    peers,
    rim,
    land,
    land_peers,
    land_rim,
    back,
    load_sem,
    store_sem,
    edge_send,
    edge_recv,
    peer_send,
    peer_recv,
    rim_send,
    rim_recv,
    land_send,
    land_recv,
    land_rim_send,
    land_rim_recv,
):
    slots, members, rows, lon, mem_count, lat_count = sizes
    groups = members // GROUP
    share = slots // mem_count
    fine_rows = 2 * rows
    me_mem = lax.axis_index("mem")
    me_lat = lax.axis_index("lat")
    has = (me_lat > 0, me_lat < lat_count - 1)
    beside = (me_lat - 1, me_lat + 1)

    loads = []

    def load(src, dst):
        loads.append(pltpu.make_async_copy(src, dst, load_sem.at[len(loads)]))
        loads[-1].start()

    load(widths_far, widths)
    for r in range(rows):
        load(control.at[:, r, :], now.at[r])
    load(source_far, source)
    load(weight_far, weight)
    own_slots = pl.ds(me_mem * share, share)
    load(obs_mask_far.at[own_slots], obs_mask)
    load(innovation_far.at[own_slots], innovation)
    for t in range(slots):
        for r in range(rows):
            load(ensemble.at[:, t, r, :], ens.at[t, r])

    mates = [lax.rem(me_mem + d, mem_count) for d in range(mem_count)]
    barrier = pltpu.get_barrier_semaphore()
    for d in range(1, mem_count):
        pl.semaphore_signal(barrier, inc=1, device_id={"mem": mates[d]}, device_id_type=MESH)
    for side in range(2):

        @pl.when(has[side])
        def _():
            for d in range(mem_count):
                pl.semaphore_signal(
                    barrier,
                    inc=1,
                    device_id={"mem": mates[d], "lat": beside[side]},
                    device_id_type=MESH,
                )

    sides = has[0].astype(jnp.int32) + has[1].astype(jnp.int32)
    pl.semaphore_wait(barrier, mem_count - 1 + mem_count * sides)

    def send_to(where, src, dst, send, recv):
        return pltpu.make_async_remote_copy(
            src_ref=src,
            dst_ref=dst,
            send_sem=send,
            recv_sem=recv,
            device_id=where,
            device_id_type=MESH,
        )

    def edge_copy(phase, side, g):
        row = 0 if side == 0 else rows - 1
        part_of = pl.ds(g * GROUP, GROUP)
        return send_to(
            {"lat": beside[side]},
            edge.at[phase, row, part_of],
            halo.at[phase, 1 - side, part_of],
            edge_send.at[phase, side, g],
            edge_recv.at[phase, 1 - side, g],
        )

    def edge_start(phase, g):
        for side in range(2):

            @pl.when(has[side])
            def _():
                edge_copy(phase, side, g).start()

    def edge_wait(phase, g):
        for side in range(2):

            @pl.when(has[side])
            def _():
                edge_copy(phase, 1 - side, g).wait_recv()

    def edge_done(phase):
        for g in range(groups):
            for side in range(2):

                @pl.when(has[side])
                def _():
                    edge_copy(phase, side, g).wait_send()

    loads[0].wait()
    weights = []
    for r in range(rows):
        width = widths[r]
        scale = jnp.float32(1.0 / (2 * WIDEST + 1))
        for w in range(WIDEST):
            scale = jnp.where(width == w, jnp.float32(1.0 / (2 * w + 1)), scale)
        weights.append(
            [jnp.where(width >= k, scale, jnp.float32(0.0)) for k in range(WIDEST + 1)]
        )

    def spread(phase, g):
        part_of = pl.ds(g * GROUP, GROUP)
        own = [edge[phase, r, part_of, :] for r in range(rows)]
        padded = [halo[phase, 0, part_of, :], *own, halo[phase, 1, part_of, :]]
        return [
            C_MID * padded[r + 1] + C_SIDE * (padded[r] + padded[r + 2]) for r in range(rows)
        ]

    for side in range(2):

        @pl.when(jnp.logical_not(has[side]))
        def _():
            for phase in range(2 * GRAD_STEPS):
                halo[phase, side] = jnp.zeros((members, lon), jnp.float32)
            for step in range(GRAD_STEPS):
                for d in range(mem_count):
                    rim[step, side, d] = jnp.zeros((share, lon), jnp.float32)
                    land_rim[step, side, d] = jnp.zeros((share, lon), jnp.float32)

    for r in range(rows):
        loads[1 + r].wait()
    for g in range(groups):
        part_of = pl.ds(g * GROUP, GROUP)
        for r in range(rows):
            edge[0, r, part_of, :] = lon_filter(now[r, part_of, :], weights[r])
        edge_start(0, g)

    early = 1 + rows + 4
    for copy in loads[1 + rows : early]:
        copy.wait()
    four = source.shape[0]
    for s in range(four):
        rows_in[pl.ds(s * fine_rows, fine_rows), :] = source[s].astype(jnp.float32)
        rows_in[pl.ds((four + s) * fine_rows, fine_rows), :] = weight[s]
    for s in range(share):
        top = (2 * four + s) * fine_rows
        rows_in[pl.ds(top, fine_rows), :] = obs_mask[s].astype(jnp.float32)
        rows_in[pl.ds(top + share * fine_rows, fine_rows), :] = innovation[s]
    line = lax.broadcasted_iota(jnp.int32, (2 * LANES, 2 * LANES), 0)
    column = lax.broadcasted_iota(jnp.int32, (2 * LANES, 2 * LANES), 1)
    wanted = jnp.where(column < LANES, 2 * column, 2 * (column - LANES) + 1)
    pick = jnp.where(line == wanted, 1.0, 0.0).astype(jnp.float32)
    for block in range(lon // LANES):
        both = jnp.dot(
            rows_in[:, pl.ds(block * 2 * LANES, 2 * LANES)],
            pick,
            precision=lax.Precision.HIGHEST,
            preferred_element_type=jnp.float32,
        )
        rows_out[0, :, pl.ds(block * LANES, LANES)] = both[:, :LANES]
        rows_out[1, :, pl.ds(block * LANES, LANES)] = both[:, LANES:]

    def both_parities(number):
        span = pl.ds(number * fine_rows, fine_rows)
        return jnp.concatenate([rows_out[0, span, :], rows_out[1, span, :]], axis=0)

    shape = (2 * fine_rows, lon)
    across = lax.broadcasted_iota(jnp.int32, shape, 1).astype(jnp.float32)
    down = lax.broadcasted_iota(jnp.int32, shape, 0).astype(jnp.float32)
    down = down - fine_rows * jnp.floor((down + 0.5) * (1.0 / fine_rows))
    parent = jnp.floor((down + 0.5) * 0.5)
    codes = []
    for s in range(four):
        flat = jnp.floor(both_parities(s) + 0.5)
        line_of = jnp.floor((flat + 0.5) * (1.0 / lon))
        shift = flat - line_of * lon - across + REACH
        shift = jnp.where(shift < 0.0, shift + lon, shift)
        shift = jnp.where(shift >= lon, shift - lon, shift)
        codes.append((line_of - parent) * COLS + shift)
    for number in range(3 * COLS):
        total = None
        for s in range(four):
            term = jnp.where(codes[s] == number, both_parities(four + s), 0.0)
            total = term if total is None else total + term
        planes[number] = total
    for s in range(share):
        mask[s] = both_parities(2 * four + s)
        target[s] = both_parities(2 * four + share + s)

    for copy in loads[early:]:
        copy.wait()

    stores = []
    for step in range(GRAD_STEPS):
        for g in range(groups):
            edge_wait(2 * step, g)
            spreads = spread(2 * step, g)
            for r in range(rows):
                forward[r, pl.ds(g * GROUP, GROUP), :] = spreads[r]
        for r in range(rows):
            for t in range(slots):
                total = jnp.zeros((GROUP, lon), jnp.float32)
                for g in range(groups):
                    part_of = pl.ds(g * GROUP, GROUP)
                    total = total + ens[t, r, part_of, :] * forward[r, part_of, :]
                total = jnp.sum(total, axis=0, keepdims=True)
                part[step, t // share, r, pl.ds(t % share, 1), :] = total

        def peer_copy(d):
            return send_to(
                {"mem": mates[d]},
                part.at[step, mates[d]],
                peers.at[step, d - 1],
                peer_send.at[step, d - 1],
                peer_recv.at[step, d - 1],
            )

        def rim_copy(side, d):
            return send_to(
                {"mem": mates[d], "lat": beside[side]},
                part.at[step, mates[d], 0 if side == 0 else rows - 1],
                rim.at[step, 1 - side, d],
                rim_send.at[step, side, d],
                rim_recv.at[step, 1 - side, d],
            )

        def land_copy(d):
            return send_to(
                {"mem": mates[d]},
                land.at[step, pl.ds(1, rows)],
                land_peers.at[step, d - 1],
                land_send.at[step, d - 1],
                land_recv.at[step, d - 1],
            )

        def land_rim_copy(side, d):
            return send_to(
                {"mem": mates[d], "lat": beside[side]},
                land.at[step, 0 if side == 0 else rows + 1],
                land_rim.at[step, 1 - side, d],
                land_rim_send.at[step, side, d],
                land_rim_recv.at[step, 1 - side, d],
            )

        def exchange(near, far):
            for side in range(2):

                @pl.when(has[side])
                def _():
                    for d in range(mem_count):
                        far(side, d).start()

            for d in range(1, mem_count):
                near(d).start()
            for d in range(1, mem_count):
                near(d).wait_recv()
            for side in range(2):

                @pl.when(has[side])
                def _():
                    for d in range(mem_count):
                        far(1 - side, d).wait_recv()

        def exchange_done(near, far):
            for d in range(1, mem_count):
                near(d).wait_send()
            for side in range(2):

                @pl.when(has[side])
                def _():
                    for d in range(mem_count):
                        far(side, d).wait_send()

        exchange(peer_copy, rim_copy)
        for s in range(share):
            lines = []
            for r in range(-1, rows + 1):
                if r < 0 or r == rows:
                    side = 0 if r < 0 else 1
                    total = rim[step, side, 0, pl.ds(s, 1), :]
                    for d in range(1, mem_count):
                        total = total + rim[step, side, d, pl.ds(s, 1), :]
                else:
                    total = part[step, me_mem, r, pl.ds(s, 1), :]
                    for d in range(1, mem_count):
                        total = total + peers[step, d - 1, r, pl.ds(s, 1), :]
                lines.append(total)
            total = None
            for near in range(3):
                stack = [
                    jnp.broadcast_to(lines[r + near], (2, lon)) for r in range(rows)
                ]
                stack = jnp.concatenate(stack * 2, axis=0)
                for col in range(COLS):
                    term = planes[near * COLS + col] * rolled(stack, REACH - col)
                    total = term if total is None else total + term
            even, odd = stencil(total[:fine_rows], total[fine_rows:])
            even = mask[s, :fine_rows, :] * (even - target[s, :fine_rows, :])
            odd = mask[s, fine_rows:, :] * (odd - target[s, fine_rows:, :])
            returned = jnp.concatenate(stencil(even, odd), axis=0)
            landed = [None] * (rows + 2)
            for near in range(3):
                total = None
                for col in range(COLS):
                    term = rolled(planes[near * COLS + col] * returned, col - REACH)
                    total = term if total is None else total + term
                total = total[:fine_rows] + total[fine_rows:]
                for r in range(rows):
                    term = total[2 * r : 2 * r + 1] + total[2 * r + 1 : 2 * r + 2]
                    before = landed[r + near]
                    landed[r + near] = term if before is None else before + term
            for r in range(rows + 2):
                land[step, r, pl.ds(s, 1), :] = landed[r]

        exchange(land_copy, land_rim_copy)
        for d in range(mem_count):
            for s in range(share):
                one = pl.ds(s, 1)
                for r in range(rows):
                    if d == 0:
                        total = land[step, r + 1, one, :]
                    else:
                        total = land_peers[step, d - 1, r, one, :]
                    if r == 0:
                        total = total + land_rim[step, 0, d, one, :]
                    if r == rows - 1:
                        total = total + land_rim[step, 1, d, one, :]
                    back[r, pl.ds(d * share + s, 1), :] = total

        slot_of = []
        for d in range(mem_count):
            owner = lax.rem(me_mem + mem_count - d, mem_count)
            slot_of.extend(owner * share + s for s in range(share))
        for g in range(groups):
            part_of = pl.ds(g * GROUP, GROUP)
            for r in range(rows):
                total = None
                for t in range(slots):
                    term = ens[slot_of[t], r, part_of, :] * back[r, pl.ds(t, 1), :]
                    total = term if total is None else total + term
                edge[2 * step + 1, r, part_of, :] = total
            edge_start(2 * step + 1, g)
        for g in range(groups):
            part_of = pl.ds(g * GROUP, GROUP)
            edge_wait(2 * step + 1, g)
            spreads = spread(2 * step + 1, g)
            for r in range(rows):
                before = now[r, part_of, :]
                after = before - STEP_SIZE * (before + lon_filter(spreads[r], weights[r]))
                if step < GRAD_STEPS - 1:
                    now[r, part_of, :] = after
                    edge[2 * step + 2, r, part_of, :] = lon_filter(after, weights[r])
                else:
                    result[r, part_of, :] = after
                    stores.append(
                        pltpu.make_async_copy(
                            result.at[r, part_of], out.at[part_of, r, :], store_sem.at[r, g]
                        )
                    )
                    stores[-1].start()
            if step < GRAD_STEPS - 1:
                edge_start(2 * step + 2, g)

        exchange_done(peer_copy, rim_copy)
        exchange_done(land_copy, land_rim_copy)

    for phase in range(2 * GRAD_STEPS):
        edge_done(phase)
    for store in stores:
        store.wait()


def local(control, ensemble, widths, source, weight, obs_mask, innovation):
    members, slots, rows, lon = ensemble.shape
    mem_count, lat_count = lax.axis_size("mem"), lax.axis_size("lat")
    phases = 2 * GRAD_STEPS
    fine_rows = 2 * rows
    share = slots // mem_count
    f32 = jnp.float32
    hbm = pl.BlockSpec(memory_space=pltpu.HBM)
    groups = members // GROUP
    stacked = 2 * source.shape[0] * fine_rows + 2 * share * fine_rows
    dma = pltpu.SemaphoreType.DMA
    return pl.pallas_call(
        functools.partial(kernel, (slots, members, rows, lon, mem_count, lat_count)),
        out_shape=jax.ShapeDtypeStruct(control.shape, f32),
        in_specs=[hbm] * 7,
        out_specs=hbm,
        scratch_shapes=[
            pltpu.SMEM(widths.shape, jnp.int32),
            pltpu.VMEM(source.shape, jnp.int32),
            pltpu.VMEM(weight.shape, f32),
            pltpu.VMEM((share, *obs_mask.shape[1:]), jnp.int32),
            pltpu.VMEM((share, *innovation.shape[1:]), f32),
            pltpu.VMEM((slots, rows, members, lon), f32),
            pltpu.VMEM((rows, members, lon), f32),
            pltpu.VMEM((phases, rows, members, lon), f32),
            pltpu.VMEM((phases, 2, members, lon), f32),
            pltpu.VMEM((rows, members, lon), f32),
            pltpu.VMEM((rows, members, lon), f32),
            pltpu.VMEM((stacked, 2 * lon), f32),
            pltpu.VMEM((2, stacked, lon), f32),
            pltpu.VMEM((3 * COLS, 2 * fine_rows, lon), f32),
            pltpu.VMEM((share, 2 * fine_rows, lon), f32),
            pltpu.VMEM((share, 2 * fine_rows, lon), f32),
            pltpu.VMEM((GRAD_STEPS, mem_count, rows, share, lon), f32),
            pltpu.VMEM((GRAD_STEPS, mem_count - 1, rows, share, lon), f32),
            pltpu.VMEM((GRAD_STEPS, 2, mem_count, share, lon), f32),
            pltpu.VMEM((GRAD_STEPS, rows + 2, share, lon), f32),
            pltpu.VMEM((GRAD_STEPS, mem_count - 1, rows, share, lon), f32),
            pltpu.VMEM((GRAD_STEPS, 2, mem_count, share, lon), f32),
            pltpu.VMEM((rows, slots, lon), f32),
            dma((5 + rows + slots * rows,)),
            dma((rows, groups)),
            dma((phases, 2, groups)),
            dma((phases, 2, groups)),
            dma((GRAD_STEPS, mem_count - 1)),
            dma((GRAD_STEPS, mem_count - 1)),
            dma((GRAD_STEPS, 2, mem_count)),
            dma((GRAD_STEPS, 2, mem_count)),
            dma((GRAD_STEPS, mem_count - 1)),
            dma((GRAD_STEPS, mem_count - 1)),
            dma((GRAD_STEPS, 2, mem_count)),
            dma((GRAD_STEPS, 2, mem_count)),
        ],
        compiler_params=pltpu.CompilerParams(
            collective_id=0, has_side_effects=True, vmem_limit_bytes=67043328
        ),
    )(widths, control, ensemble, source, weight, obs_mask, innovation)


def solution(mesh):
    in_specs = (
        P("mem", "lat", None),
        P("mem", None, "lat", None),
        P("lat"),
        P(None, "lat", None),
        P(None, "lat", None),
        P(None, "lat", None),
        P(None, "lat", None),
    )
    out_specs = P("mem", "lat", None)
    return jax.shard_map(local, mesh=mesh, in_specs=in_specs, out_specs=out_specs, check_vma=False)
```

```python
import functools

import jax
import jax.numpy as jnp
from jax import lax
from jax.experimental import pallas as pl
from jax.experimental.pallas import tpu as pltpu
from jax.sharding import PartitionSpec as P

WIDEST = 4
GRAD_STEPS = 2
C_MID = 0.5
C_SIDE = 0.25
STEP_SIZE = 0.5
GROUP = 8
LANES = 128
REACH = 2
COLS = 2 * REACH + 1
MESH = pl.DeviceIdType.MESH


def rolled(x, shift):
    shift = shift % x.shape[-1]
    return x if shift == 0 else pltpu.roll(x, shift, x.ndim - 1)


def lon_filter(x, weights):
    total = x * weights[0]
    for k in range(1, WIDEST + 1):
        total = total + (rolled(x, k) + rolled(x, -k)) * weights[k]
    return total


def stencil(even, odd):
    return (
        0.25 * (rolled(odd, 1) + odd) + 0.5 * even,
        0.25 * (even + rolled(even, -1)) + 0.5 * odd,
    )


def kernel(
    sizes,
    widths_far,
    control,
    ensemble,
    source_far,
    weight_far,
    obs_mask_far,
    innovation_far,
    out,
    widths,
    source,
    weight,
    obs_mask,
    innovation,
    ens,
    now,
    edge,
    halo,
    sums,
    result,
    rows_in,
    rows_out,
    planes,
    mask,
    target,
    part,
    peers,
    rim,
    land,
    land_peers,
    land_rim,
    back,
    load_sem,
    store_sem,
    edge_send,
    edge_recv,
    peer_send,
    peer_recv,
    rim_send,
    rim_recv,
    land_send,
    land_recv,
    land_rim_send,
    land_rim_recv,
):
    slots, members, rows, lon, mem_count, lat_count = sizes
    groups = members // GROUP
    share = slots // mem_count
    fine_rows = 2 * rows
    me_mem = lax.axis_index("mem")
    me_lat = lax.axis_index("lat")
    has = (me_lat > 0, me_lat < lat_count - 1)
    beside = (me_lat - 1, me_lat + 1)

    loads = []

    def load(src, dst):
        loads.append(pltpu.make_async_copy(src, dst, load_sem.at[len(loads)]))
        loads[-1].start()

    load(widths_far, widths)
    for g in range(groups):
        for r in range(rows):
            part_of = pl.ds(g * GROUP, GROUP)
            load(control.at[part_of, r, :], now.at[r, part_of])
    load(source_far, source)
    load(weight_far, weight)
    own_slots = pl.ds(me_mem * share, share)
    load(obs_mask_far.at[own_slots], obs_mask)
    load(innovation_far.at[own_slots], innovation)
    for t in range(slots):
        for r in range(rows):
            load(ensemble.at[:, t, r, :], ens.at[t, r])

    mates = [lax.rem(me_mem + d, mem_count) for d in range(mem_count)]
    barrier = pltpu.get_barrier_semaphore()
    for d in range(1, mem_count):
        pl.semaphore_signal(barrier, inc=1, device_id={"mem": mates[d]}, device_id_type=MESH)
    for side in range(2):

        @pl.when(has[side])
        def _():
            for d in range(mem_count):
                pl.semaphore_signal(
                    barrier,
                    inc=1,
                    device_id={"mem": mates[d], "lat": beside[side]},
                    device_id_type=MESH,
                )

    sides = has[0].astype(jnp.int32) + has[1].astype(jnp.int32)
    pl.semaphore_wait(barrier, mem_count - 1 + mem_count * sides)

    def send_to(where, src, dst, send, recv):
        return pltpu.make_async_remote_copy(
            src_ref=src,
            dst_ref=dst,
            send_sem=send,
            recv_sem=recv,
            device_id=where,
            device_id_type=MESH,
        )

    def edge_copy(phase, side, g):
        row = 0 if side == 0 else rows - 1
        part_of = pl.ds(g * GROUP, GROUP)
        return send_to(
            {"lat": beside[side]},
            edge.at[phase, row, part_of],
            halo.at[phase, 1 - side, part_of],
            edge_send.at[phase, side, g],
            edge_recv.at[phase, 1 - side, g],
        )

    def edge_start(phase, g):
        for side in range(2):

            @pl.when(has[side])
            def _():
                edge_copy(phase, side, g).start()

    def edge_wait(phase, g):
        for side in range(2):

            @pl.when(has[side])
            def _():
                edge_copy(phase, 1 - side, g).wait_recv()

    def edge_done(phase):
        for g in range(groups):
            for side in range(2):

                @pl.when(has[side])
                def _():
                    edge_copy(phase, side, g).wait_send()

    loads[0].wait()
    weights = []
    for r in range(rows):
        width = widths[r]
        scale = jnp.float32(1.0 / (2 * WIDEST + 1))
        for w in range(WIDEST):
            scale = jnp.where(width == w, jnp.float32(1.0 / (2 * w + 1)), scale)
        weights.append(
            [jnp.where(width >= k, scale, jnp.float32(0.0)) for k in range(WIDEST + 1)]
        )

    def spread(phase, g):
        part_of = pl.ds(g * GROUP, GROUP)
        own = [edge[phase, r, part_of, :] for r in range(rows)]
        padded = [halo[phase, 0, part_of, :], *own, halo[phase, 1, part_of, :]]
        return [
            C_MID * padded[r + 1] + C_SIDE * (padded[r] + padded[r + 2]) for r in range(rows)
        ]

    for side in range(2):

        @pl.when(jnp.logical_not(has[side]))
        def _():
            for phase in range(2 * GRAD_STEPS):
                halo[phase, side] = jnp.zeros((members, lon), jnp.float32)
            for step in range(GRAD_STEPS):
                for d in range(mem_count):
                    rim[step, side, d] = jnp.zeros((share, lon), jnp.float32)
                    land_rim[step, side, d] = jnp.zeros((share, lon), jnp.float32)

    for g in range(groups):
        part_of = pl.ds(g * GROUP, GROUP)
        for r in range(rows):
            loads[1 + g * rows + r].wait()
            edge[0, r, part_of, :] = lon_filter(now[r, part_of, :], weights[r])
        edge_start(0, g)

    early = 1 + groups * rows + 4
    for copy in loads[early - 4 : early]:
        copy.wait()
    four = source.shape[0]
    for s in range(four):
        rows_in[pl.ds(s * fine_rows, fine_rows), :] = source[s].astype(jnp.float32)
        rows_in[pl.ds((four + s) * fine_rows, fine_rows), :] = weight[s]
    for s in range(share):
        top = (2 * four + s) * fine_rows
        rows_in[pl.ds(top, fine_rows), :] = obs_mask[s].astype(jnp.float32)
        rows_in[pl.ds(top + share * fine_rows, fine_rows), :] = innovation[s]
    line = lax.broadcasted_iota(jnp.int32, (2 * LANES, 2 * LANES), 0)
    column = lax.broadcasted_iota(jnp.int32, (2 * LANES, 2 * LANES), 1)
    wanted = jnp.where(column < LANES, 2 * column, 2 * (column - LANES) + 1)
    pick = jnp.where(line == wanted, 1.0, 0.0).astype(jnp.float32)
    for block in range(lon // LANES):
        both = jnp.dot(
            rows_in[:, pl.ds(block * 2 * LANES, 2 * LANES)],
            pick,
            precision=lax.Precision.HIGHEST,
            preferred_element_type=jnp.float32,
        )
        rows_out[0, :, pl.ds(block * LANES, LANES)] = both[:, :LANES]
        rows_out[1, :, pl.ds(block * LANES, LANES)] = both[:, LANES:]

    def both_parities(number):
        span = pl.ds(number * fine_rows, fine_rows)
        return jnp.concatenate([rows_out[0, span, :], rows_out[1, span, :]], axis=0)

    shape = (2 * fine_rows, lon)
    across = lax.broadcasted_iota(jnp.int32, shape, 1).astype(jnp.float32)
    down = lax.broadcasted_iota(jnp.int32, shape, 0).astype(jnp.float32)
    down = down - fine_rows * jnp.floor((down + 0.5) * (1.0 / fine_rows))
    parent = jnp.floor((down + 0.5) * 0.5)
    codes = []
    for s in range(four):
        flat = jnp.floor(both_parities(s) + 0.5)
        line_of = jnp.floor((flat + 0.5) * (1.0 / lon))
        shift = flat - line_of * lon - across + REACH
        shift = jnp.where(shift < 0.0, shift + lon, shift)
        shift = jnp.where(shift >= lon, shift - lon, shift)
        codes.append((line_of - parent) * COLS + shift)
    for number in range(3 * COLS):
        total = None
        for s in range(four):
            term = jnp.where(codes[s] == number, both_parities(four + s), 0.0)
            total = term if total is None else total + term
        planes[number] = total
    for s in range(share):
        mask[s] = both_parities(2 * four + s)
        target[s] = both_parities(2 * four + share + s)

    for copy in loads[early:]:
        copy.wait()

    stores = []
    for step in range(GRAD_STEPS):
        for g in range(groups):
            edge_wait(2 * step, g)
            spreads = spread(2 * step, g)
            part_of = pl.ds(g * GROUP, GROUP)
            for r in range(rows):
                for t in range(slots):
                    term = ens[t, r, part_of, :] * spreads[r]
                    sums[r, t] = term if g == 0 else sums[r, t] + term
        for r in range(rows):
            for t in range(slots):
                total = jnp.sum(sums[r, t], axis=0, keepdims=True)
                part[step, t // share, r, pl.ds(t % share, 1), :] = total

        def peer_copy(d):
            return send_to(
                {"mem": mates[d]},
                part.at[step, mates[d]],
                peers.at[step, d - 1],
                peer_send.at[step, d - 1],
                peer_recv.at[step, d - 1],
            )

        def rim_copy(side, d):
            return send_to(
                {"mem": mates[d], "lat": beside[side]},
                part.at[step, mates[d], 0 if side == 0 else rows - 1],
                rim.at[step, 1 - side, d],
                rim_send.at[step, side, d],
                rim_recv.at[step, 1 - side, d],
            )

        def land_copy(d):
            return send_to(
                {"mem": mates[d]},
                land.at[step, pl.ds(1, rows)],
                land_peers.at[step, d - 1],
                land_send.at[step, d - 1],
                land_recv.at[step, d - 1],
            )

        def land_rim_copy(side, d):
            return send_to(
                {"mem": mates[d], "lat": beside[side]},
                land.at[step, 0 if side == 0 else rows + 1],
                land_rim.at[step, 1 - side, d],
                land_rim_send.at[step, side, d],
                land_rim_recv.at[step, 1 - side, d],
            )

        def exchange(near, far):
            for side in range(2):

                @pl.when(has[side])
                def _():
                    for d in range(mem_count):
                        far(side, d).start()

            for d in range(1, mem_count):
                near(d).start()
            for d in range(1, mem_count):
                near(d).wait_recv()
            for side in range(2):

                @pl.when(has[side])
                def _():
                    for d in range(mem_count):
                        far(1 - side, d).wait_recv()

        def exchange_done(near, far):
            for d in range(1, mem_count):
                near(d).wait_send()
            for side in range(2):

                @pl.when(has[side])
                def _():
                    for d in range(mem_count):
                        far(side, d).wait_send()

        exchange(peer_copy, rim_copy)
        for s in range(share):
            lines = []
            for r in range(-1, rows + 1):
                if r < 0 or r == rows:
                    side = 0 if r < 0 else 1
                    total = rim[step, side, 0, pl.ds(s, 1), :]
                    for d in range(1, mem_count):
                        total = total + rim[step, side, d, pl.ds(s, 1), :]
                else:
                    total = part[step, me_mem, r, pl.ds(s, 1), :]
                    for d in range(1, mem_count):
                        total = total + peers[step, d - 1, r, pl.ds(s, 1), :]
                lines.append(total)
            total = None
            for near in range(3):
                stack = [
                    jnp.broadcast_to(lines[r + near], (2, lon)) for r in range(rows)
                ]
                stack = jnp.concatenate(stack * 2, axis=0)
                for col in range(COLS):
                    term = planes[near * COLS + col] * rolled(stack, REACH - col)
                    total = term if total is None else total + term
            even, odd = stencil(total[:fine_rows], total[fine_rows:])
            even = mask[s, :fine_rows, :] * (even - target[s, :fine_rows, :])
            odd = mask[s, fine_rows:, :] * (odd - target[s, fine_rows:, :])
            returned = jnp.concatenate(stencil(even, odd), axis=0)
            landed = [None] * (rows + 2)
            for near in range(3):
                total = None
                for col in range(COLS):
                    term = rolled(planes[near * COLS + col] * returned, col - REACH)
                    total = term if total is None else total + term
                total = total[:fine_rows] + total[fine_rows:]
                for r in range(rows):
                    term = total[2 * r : 2 * r + 1] + total[2 * r + 1 : 2 * r + 2]
                    before = landed[r + near]
                    landed[r + near] = term if before is None else before + term
            for r in range(rows + 2):
                land[step, r, pl.ds(s, 1), :] = landed[r]

        exchange(land_copy, land_rim_copy)
        for d in range(mem_count):
            for s in range(share):
                one = pl.ds(s, 1)
                for r in range(rows):
                    if d == 0:
                        total = land[step, r + 1, one, :]
                    else:
                        total = land_peers[step, d - 1, r, one, :]
                    if r == 0:
                        total = total + land_rim[step, 0, d, one, :]
                    if r == rows - 1:
                        total = total + land_rim[step, 1, d, one, :]
                    back[r, pl.ds(d * share + s, 1), :] = total

        slot_of = []
        for d in range(mem_count):
            owner = lax.rem(me_mem + mem_count - d, mem_count)
            slot_of.extend(owner * share + s for s in range(share))
        for g in range(groups):
            part_of = pl.ds(g * GROUP, GROUP)
            for r in range(rows):
                total = None
                for t in range(slots):
                    term = ens[slot_of[t], r, part_of, :] * back[r, pl.ds(t, 1), :]
                    total = term if total is None else total + term
                edge[2 * step + 1, r, part_of, :] = total
            edge_start(2 * step + 1, g)
        for g in range(groups):
            part_of = pl.ds(g * GROUP, GROUP)
            edge_wait(2 * step + 1, g)
            spreads = spread(2 * step + 1, g)
            for r in range(rows):
                before = now[r, part_of, :]
                after = before - STEP_SIZE * (before + lon_filter(spreads[r], weights[r]))
                if step < GRAD_STEPS - 1:
                    now[r, part_of, :] = after
                    edge[2 * step + 2, r, part_of, :] = lon_filter(after, weights[r])
                else:
                    result[r, part_of, :] = after
                    stores.append(
                        pltpu.make_async_copy(
                            result.at[r, part_of], out.at[part_of, r, :], store_sem.at[r, g]
                        )
                    )
                    stores[-1].start()
            if step < GRAD_STEPS - 1:
                edge_start(2 * step + 2, g)

        exchange_done(peer_copy, rim_copy)
        exchange_done(land_copy, land_rim_copy)

    for phase in range(2 * GRAD_STEPS):
        edge_done(phase)
    for store in stores:
        store.wait()


def local(control, ensemble, widths, source, weight, obs_mask, innovation):
    members, slots, rows, lon = ensemble.shape
    mem_count, lat_count = lax.axis_size("mem"), lax.axis_size("lat")
    phases = 2 * GRAD_STEPS
    fine_rows = 2 * rows
    share = slots // mem_count
    f32 = jnp.float32
    hbm = pl.BlockSpec(memory_space=pltpu.HBM)
    groups = members // GROUP
    stacked = 2 * source.shape[0] * fine_rows + 2 * share * fine_rows
    dma = pltpu.SemaphoreType.DMA
    return pl.pallas_call(
        functools.partial(kernel, (slots, members, rows, lon, mem_count, lat_count)),
        out_shape=jax.ShapeDtypeStruct(control.shape, f32),
        in_specs=[hbm] * 7,
        out_specs=pl.BlockSpec(memory_space=pl.ANY),
        scratch_shapes=[
            pltpu.SMEM(widths.shape, jnp.int32),
            pltpu.VMEM(source.shape, jnp.int32),
            pltpu.VMEM(weight.shape, f32),
            pltpu.VMEM((share, *obs_mask.shape[1:]), jnp.int32),
            pltpu.VMEM((share, *innovation.shape[1:]), f32),
            pltpu.VMEM((slots, rows, members, lon), f32),
            pltpu.VMEM((rows, members, lon), f32),
            pltpu.VMEM((phases, rows, members, lon), f32),
            pltpu.VMEM((phases, 2, members, lon), f32),
            pltpu.VMEM((rows, slots, GROUP, lon), f32),
            pltpu.VMEM((rows, members, lon), f32),
            pltpu.VMEM((stacked, 2 * lon), f32),
            pltpu.VMEM((2, stacked, lon), f32),
            pltpu.VMEM((3 * COLS, 2 * fine_rows, lon), f32),
            pltpu.VMEM((share, 2 * fine_rows, lon), f32),
            pltpu.VMEM((share, 2 * fine_rows, lon), f32),
            pltpu.VMEM((GRAD_STEPS, mem_count, rows, share, lon), f32),
            pltpu.VMEM((GRAD_STEPS, mem_count - 1, rows, share, lon), f32),
            pltpu.VMEM((GRAD_STEPS, 2, mem_count, share, lon), f32),
            pltpu.VMEM((GRAD_STEPS, rows + 2, share, lon), f32),
            pltpu.VMEM((GRAD_STEPS, mem_count - 1, rows, share, lon), f32),
            pltpu.VMEM((GRAD_STEPS, 2, mem_count, share, lon), f32),
            pltpu.VMEM((rows, slots, lon), f32),
            dma((5 + groups * rows + slots * rows,)),
            dma((rows, groups)),
            dma((phases, 2, groups)),
            dma((phases, 2, groups)),
            dma((GRAD_STEPS, mem_count - 1)),
            dma((GRAD_STEPS, mem_count - 1)),
            dma((GRAD_STEPS, 2, mem_count)),
            dma((GRAD_STEPS, 2, mem_count)),
            dma((GRAD_STEPS, mem_count - 1)),
            dma((GRAD_STEPS, mem_count - 1)),
            dma((GRAD_STEPS, 2, mem_count)),
            dma((GRAD_STEPS, 2, mem_count)),
        ],
        compiler_params=pltpu.CompilerParams(
            collective_id=0, has_side_effects=True, vmem_limit_bytes=48 * 1024 * 1024
        ),
    )(
        *[
            pltpu.with_memory_space_constraint(x, pltpu.HBM)
            for x in (widths, control, ensemble, source, weight, obs_mask, innovation)
        ]
    )


def solution(mesh):
    in_specs = (
        P("mem", "lat", None),
        P("mem", None, "lat", None),
        P("lat"),
        P(None, "lat", None),
        P(None, "lat", None),
        P(None, "lat", None),
        P(None, "lat", None),
    )
    out_specs = P("mem", "lat", None)
    return jax.shard_map(local, mesh=mesh, in_specs=in_specs, out_specs=out_specs, check_vma=False)
```

```python
import functools

import jax
import jax.numpy as jnp
from jax import lax
from jax.experimental import pallas as pl
from jax.experimental.pallas import tpu as pltpu
from jax.sharding import PartitionSpec as P

WIDEST = 4
GRAD_STEPS = 2
C_MID = 0.5
C_SIDE = 0.25
STEP_SIZE = 0.5
GROUP = 8
LANES = 128
REACH = 2
COLS = 2 * REACH + 1
MESH = pl.DeviceIdType.MESH


def rolled(x, shift):
    shift = shift % x.shape[-1]
    return x if shift == 0 else pltpu.roll(x, shift, x.ndim - 1)


def lon_filter(x, weights):
    total = x * weights[0]
    for k in range(1, WIDEST + 1):
        total = total + (rolled(x, k) + rolled(x, -k)) * weights[k]
    return total


def stencil(even, odd):
    return (
        0.25 * (rolled(odd, 1) + odd) + 0.5 * even,
        0.25 * (even + rolled(even, -1)) + 0.5 * odd,
    )


def kernel(
    sizes,
    widths_far,
    control,
    ensemble,
    source_far,
    weight_far,
    obs_mask_far,
    innovation_far,
    out,
    widths,
    source,
    weight,
    obs_mask,
    innovation,
    ens,
    now,
    edge,
    halo,
    sums,
    result,
    rows_in,
    rows_out,
    planes,
    mask,
    target,
    part,
    peers,
    rim,
    land,
    land_peers,
    land_rim,
    back,
    load_sem,
    store_sem,
    edge_send,
    edge_recv,
    peer_send,
    peer_recv,
    rim_send,
    rim_recv,
    land_send,
    land_recv,
    land_rim_send,
    land_rim_recv,
):
    slots, members, rows, lon, mem_count, lat_count = sizes
    groups = members // GROUP
    share = slots // mem_count
    fine_rows = 2 * rows
    me_mem = lax.axis_index("mem")
    me_lat = lax.axis_index("lat")
    has = (me_lat > 0, me_lat < lat_count - 1)
    beside = (me_lat - 1, me_lat + 1)

    mates = [lax.rem(me_mem + d, mem_count) for d in range(mem_count)]
    barrier = pltpu.get_barrier_semaphore()
    for d in range(1, mem_count):
        pl.semaphore_signal(barrier, inc=1, device_id={"mem": mates[d]}, device_id_type=MESH)
    for side in range(2):

        @pl.when(has[side])
        def _():
            for d in range(mem_count):
                pl.semaphore_signal(
                    barrier,
                    inc=1,
                    device_id={"mem": mates[d], "lat": beside[side]},
                    device_id_type=MESH,
                )

    sides = has[0].astype(jnp.int32) + has[1].astype(jnp.int32)
    loads = []

    def load(src, dst):
        loads.append(pltpu.make_async_copy(src, dst, load_sem.at[len(loads)]))
        loads[-1].start()

    load(widths_far, widths)
    for g in range(groups):
        for r in range(rows):
            part_of = pl.ds(g * GROUP, GROUP)
            load(control.at[part_of, r, :], now.at[r, part_of])
    load(source_far, source)
    load(weight_far, weight)
    own_slots = pl.ds(me_mem * share, share)
    load(obs_mask_far.at[own_slots], obs_mask)
    load(innovation_far.at[own_slots], innovation)
    for t in range(slots):
        for r in range(rows):
            load(ensemble.at[:, t, r, :], ens.at[t, r])

    def send_to(where, src, dst, send, recv):
        return pltpu.make_async_remote_copy(
            src_ref=src,
            dst_ref=dst,
            send_sem=send,
            recv_sem=recv,
            device_id=where,
            device_id_type=MESH,
        )

    def edge_copy(phase, side, g):
        row = 0 if side == 0 else rows - 1
        part_of = pl.ds(g * GROUP, GROUP)
        return send_to(
            {"lat": beside[side]},
            edge.at[phase, row, part_of],
            halo.at[phase, 1 - side, part_of],
            edge_send.at[phase, side, g],
            edge_recv.at[phase, 1 - side, g],
        )

    def edge_start(phase, g):
        for side in range(2):

            @pl.when(has[side])
            def _():
                edge_copy(phase, side, g).start()

    def edge_wait(phase, g):
        for side in range(2):

            @pl.when(has[side])
            def _():
                edge_copy(phase, 1 - side, g).wait_recv()

    def edge_done(phase):
        for g in range(groups):
            for side in range(2):

                @pl.when(has[side])
                def _():
                    edge_copy(phase, side, g).wait_send()

    loads[0].wait()
    weights = []
    for r in range(rows):
        width = widths[r]
        scale = jnp.float32(1.0 / (2 * WIDEST + 1))
        for w in range(WIDEST):
            scale = jnp.where(width == w, jnp.float32(1.0 / (2 * w + 1)), scale)
        weights.append(
            [jnp.where(width >= k, scale, jnp.float32(0.0)) for k in range(WIDEST + 1)]
        )

    def spread(phase, g):
        part_of = pl.ds(g * GROUP, GROUP)
        own = [edge[phase, r, part_of, :] for r in range(rows)]
        padded = [halo[phase, 0, part_of, :], *own, halo[phase, 1, part_of, :]]
        return [
            C_MID * padded[r + 1] + C_SIDE * (padded[r] + padded[r + 2]) for r in range(rows)
        ]

    for side in range(2):

        @pl.when(jnp.logical_not(has[side]))
        def _():
            for phase in range(2 * GRAD_STEPS):
                halo[phase, side] = jnp.zeros((members, lon), jnp.float32)
            for step in range(GRAD_STEPS):
                for d in range(mem_count):
                    rim[step, side, d] = jnp.zeros((share, lon), jnp.float32)
                    land_rim[step, side, d] = jnp.zeros((share, lon), jnp.float32)

    for g in range(groups):
        part_of = pl.ds(g * GROUP, GROUP)
        for r in range(rows):
            loads[1 + g * rows + r].wait()
            edge[0, r, part_of, :] = lon_filter(now[r, part_of, :], weights[r])
        if g == 0:
            pl.semaphore_wait(barrier, mem_count - 1 + mem_count * sides)
        edge_start(0, g)

    early = 1 + groups * rows + 4
    for copy in loads[early - 4 : early]:
        copy.wait()
    four = source.shape[0]
    for s in range(four):
        rows_in[pl.ds(s * fine_rows, fine_rows), :] = source[s].astype(jnp.float32)
        rows_in[pl.ds((four + s) * fine_rows, fine_rows), :] = weight[s]
    for s in range(share):
        top = (2 * four + s) * fine_rows
        rows_in[pl.ds(top, fine_rows), :] = obs_mask[s].astype(jnp.float32)
        rows_in[pl.ds(top + share * fine_rows, fine_rows), :] = innovation[s]
    line = lax.broadcasted_iota(jnp.int32, (2 * LANES, 2 * LANES), 0)
    column = lax.broadcasted_iota(jnp.int32, (2 * LANES, 2 * LANES), 1)
    wanted = jnp.where(column < LANES, 2 * column, 2 * (column - LANES) + 1)
    pick = jnp.where(line == wanted, 1.0, 0.0).astype(jnp.float32)
    for block in range(lon // LANES):
        both = jnp.dot(
            rows_in[:, pl.ds(block * 2 * LANES, 2 * LANES)],
            pick,
            precision=lax.Precision.HIGHEST,
            preferred_element_type=jnp.float32,
        )
        rows_out[0, :, pl.ds(block * LANES, LANES)] = both[:, :LANES]
        rows_out[1, :, pl.ds(block * LANES, LANES)] = both[:, LANES:]

    def both_parities(number):
        span = pl.ds(number * fine_rows, fine_rows)
        return jnp.concatenate([rows_out[0, span, :], rows_out[1, span, :]], axis=0)

    shape = (2 * fine_rows, lon)
    across = lax.broadcasted_iota(jnp.int32, shape, 1).astype(jnp.float32)
    down = lax.broadcasted_iota(jnp.int32, shape, 0).astype(jnp.float32)
    down = down - fine_rows * jnp.floor((down + 0.5) * (1.0 / fine_rows))
    parent = jnp.floor((down + 0.5) * 0.5)
    codes = []
    for s in range(four):
        flat = jnp.floor(both_parities(s) + 0.5)
        line_of = jnp.floor((flat + 0.5) * (1.0 / lon))
        shift = flat - line_of * lon - across + REACH
        shift = jnp.where(shift < 0.0, shift + lon, shift)
        shift = jnp.where(shift >= lon, shift - lon, shift)
        codes.append((line_of - parent) * COLS + shift)
    for number in range(3 * COLS):
        total = None
        for s in range(four):
            term = jnp.where(codes[s] == number, both_parities(four + s), 0.0)
            total = term if total is None else total + term
        planes[number] = total
    for s in range(share):
        mask[s] = both_parities(2 * four + s)
        target[s] = both_parities(2 * four + share + s)

    for copy in loads[early:]:
        copy.wait()

    stores = []
    for step in range(GRAD_STEPS):
        for g in range(groups):
            edge_wait(2 * step, g)
            spreads = spread(2 * step, g)
            part_of = pl.ds(g * GROUP, GROUP)
            for r in range(rows):
                for t in range(slots):
                    term = ens[t, r, part_of, :] * spreads[r]
                    sums[r, t] = term if g == 0 else sums[r, t] + term
        for r in range(rows):
            for t in range(slots):
                total = jnp.sum(sums[r, t], axis=0, keepdims=True)
                part[step, t // share, r, pl.ds(t % share, 1), :] = total

        def peer_copy(d):
            return send_to(
                {"mem": mates[d]},
                part.at[step, mates[d]],
                peers.at[step, d - 1],
                peer_send.at[step, d - 1],
                peer_recv.at[step, d - 1],
            )

        def rim_copy(side, d):
            return send_to(
                {"mem": mates[d], "lat": beside[side]},
                part.at[step, mates[d], 0 if side == 0 else rows - 1],
                rim.at[step, 1 - side, d],
                rim_send.at[step, side, d],
                rim_recv.at[step, 1 - side, d],
            )

        def land_copy(d):
            return send_to(
                {"mem": mates[d]},
                land.at[step, pl.ds(1, rows)],
                land_peers.at[step, d - 1],
                land_send.at[step, d - 1],
                land_recv.at[step, d - 1],
            )

        def land_rim_copy(side, d):
            return send_to(
                {"mem": mates[d], "lat": beside[side]},
                land.at[step, 0 if side == 0 else rows + 1],
                land_rim.at[step, 1 - side, d],
                land_rim_send.at[step, side, d],
                land_rim_recv.at[step, 1 - side, d],
            )

        def exchange(near, far):
            for side in range(2):

                @pl.when(has[side])
                def _():
                    for d in range(mem_count):
                        far(side, d).start()

            for d in range(1, mem_count):
                near(d).start()
            for d in range(1, mem_count):
                near(d).wait_recv()
            for side in range(2):

                @pl.when(has[side])
                def _():
                    for d in range(mem_count):
                        far(1 - side, d).wait_recv()

        def exchange_done(near, far):
            for d in range(1, mem_count):
                near(d).wait_send()
            for side in range(2):

                @pl.when(has[side])
                def _():
                    for d in range(mem_count):
                        far(side, d).wait_send()

        exchange(peer_copy, rim_copy)
        for s in range(share):
            lines = []
            for r in range(-1, rows + 1):
                if r < 0 or r == rows:
                    side = 0 if r < 0 else 1
                    total = rim[step, side, 0, pl.ds(s, 1), :]
                    for d in range(1, mem_count):
                        total = total + rim[step, side, d, pl.ds(s, 1), :]
                else:
                    total = part[step, me_mem, r, pl.ds(s, 1), :]
                    for d in range(1, mem_count):
                        total = total + peers[step, d - 1, r, pl.ds(s, 1), :]
                lines.append(total)
            total = None
            for near in range(3):
                stack = [
                    jnp.broadcast_to(lines[r + near], (2, lon)) for r in range(rows)
                ]
                stack = jnp.concatenate(stack * 2, axis=0)
                for col in range(COLS):
                    term = planes[near * COLS + col] * rolled(stack, REACH - col)
                    total = term if total is None else total + term
            even, odd = stencil(total[:fine_rows], total[fine_rows:])
            even = mask[s, :fine_rows, :] * (even - target[s, :fine_rows, :])
            odd = mask[s, fine_rows:, :] * (odd - target[s, fine_rows:, :])
            returned = jnp.concatenate(stencil(even, odd), axis=0)
            landed = [None] * (rows + 2)
            for near in range(3):
                total = None
                for col in range(COLS):
                    term = rolled(planes[near * COLS + col] * returned, col - REACH)
                    total = term if total is None else total + term
                total = total[:fine_rows] + total[fine_rows:]
                for r in range(rows):
                    term = total[2 * r : 2 * r + 1] + total[2 * r + 1 : 2 * r + 2]
                    before = landed[r + near]
                    landed[r + near] = term if before is None else before + term
            for r in range(rows + 2):
                land[step, r, pl.ds(s, 1), :] = landed[r]

        exchange(land_copy, land_rim_copy)
        for d in range(mem_count):
            for s in range(share):
                one = pl.ds(s, 1)
                for r in range(rows):
                    if d == 0:
                        total = land[step, r + 1, one, :]
                    else:
                        total = land_peers[step, d - 1, r, one, :]
                    if r == 0:
                        total = total + land_rim[step, 0, d, one, :]
                    if r == rows - 1:
                        total = total + land_rim[step, 1, d, one, :]
                    back[r, pl.ds(d * share + s, 1), :] = total

        slot_of = []
        for d in range(mem_count):
            owner = lax.rem(me_mem + mem_count - d, mem_count)
            slot_of.extend(owner * share + s for s in range(share))
        for g in range(groups):
            part_of = pl.ds(g * GROUP, GROUP)
            for r in range(rows):
                total = None
                for t in range(slots):
                    term = ens[slot_of[t], r, part_of, :] * back[r, pl.ds(t, 1), :]
                    total = term if total is None else total + term
                edge[2 * step + 1, r, part_of, :] = total
            edge_start(2 * step + 1, g)
        for g in range(groups):
            part_of = pl.ds(g * GROUP, GROUP)
            edge_wait(2 * step + 1, g)
            spreads = spread(2 * step + 1, g)
            for r in range(rows):
                before = now[r, part_of, :]
                after = before - STEP_SIZE * (before + lon_filter(spreads[r], weights[r]))
                if step < GRAD_STEPS - 1:
                    now[r, part_of, :] = after
                    edge[2 * step + 2, r, part_of, :] = lon_filter(after, weights[r])
                else:
                    result[r, part_of, :] = after
                    stores.append(
                        pltpu.make_async_copy(
                            result.at[r, part_of], out.at[part_of, r, :], store_sem.at[r, g]
                        )
                    )
                    stores[-1].start()
            if step < GRAD_STEPS - 1:
                edge_start(2 * step + 2, g)

        exchange_done(peer_copy, rim_copy)
        exchange_done(land_copy, land_rim_copy)

    for phase in range(2 * GRAD_STEPS):
        edge_done(phase)
    for store in stores:
        store.wait()


def local(control, ensemble, widths, source, weight, obs_mask, innovation):
    members, slots, rows, lon = ensemble.shape
    mem_count, lat_count = lax.axis_size("mem"), lax.axis_size("lat")
    phases = 2 * GRAD_STEPS
    fine_rows = 2 * rows
    share = slots // mem_count
    f32 = jnp.float32
    hbm = pl.BlockSpec(memory_space=pltpu.HBM)
    groups = members // GROUP
    stacked = 2 * source.shape[0] * fine_rows + 2 * share * fine_rows
    dma = pltpu.SemaphoreType.DMA
    return pl.pallas_call(
        functools.partial(kernel, (slots, members, rows, lon, mem_count, lat_count)),
        out_shape=jax.ShapeDtypeStruct(control.shape, f32),
        in_specs=[hbm] * 7,
        out_specs=pl.BlockSpec(memory_space=pl.ANY),
        scratch_shapes=[
            pltpu.SMEM(widths.shape, jnp.int32),
            pltpu.VMEM(source.shape, jnp.int32),
            pltpu.VMEM(weight.shape, f32),
            pltpu.VMEM((share, *obs_mask.shape[1:]), jnp.int32),
            pltpu.VMEM((share, *innovation.shape[1:]), f32),
            pltpu.VMEM((slots, rows, members, lon), f32),
            pltpu.VMEM((rows, members, lon), f32),
            pltpu.VMEM((phases, rows, members, lon), f32),
            pltpu.VMEM((phases, 2, members, lon), f32),
            pltpu.VMEM((rows, slots, GROUP, lon), f32),
            pltpu.VMEM((rows, members, lon), f32),
            pltpu.VMEM((stacked, 2 * lon), f32),
            pltpu.VMEM((2, stacked, lon), f32),
            pltpu.VMEM((3 * COLS, 2 * fine_rows, lon), f32),
            pltpu.VMEM((share, 2 * fine_rows, lon), f32),
            pltpu.VMEM((share, 2 * fine_rows, lon), f32),
            pltpu.VMEM((GRAD_STEPS, mem_count, rows, share, lon), f32),
            pltpu.VMEM((GRAD_STEPS, mem_count - 1, rows, share, lon), f32),
            pltpu.VMEM((GRAD_STEPS, 2, mem_count, share, lon), f32),
            pltpu.VMEM((GRAD_STEPS, rows + 2, share, lon), f32),
            pltpu.VMEM((GRAD_STEPS, mem_count - 1, rows, share, lon), f32),
            pltpu.VMEM((GRAD_STEPS, 2, mem_count, share, lon), f32),
            pltpu.VMEM((rows, slots, lon), f32),
            dma((5 + groups * rows + slots * rows,)),
            dma((rows, groups)),
            dma((phases, 2, groups)),
            dma((phases, 2, groups)),
            dma((GRAD_STEPS, mem_count - 1)),
            dma((GRAD_STEPS, mem_count - 1)),
            dma((GRAD_STEPS, 2, mem_count)),
            dma((GRAD_STEPS, 2, mem_count)),
            dma((GRAD_STEPS, mem_count - 1)),
            dma((GRAD_STEPS, mem_count - 1)),
            dma((GRAD_STEPS, 2, mem_count)),
            dma((GRAD_STEPS, 2, mem_count)),
        ],
        compiler_params=pltpu.CompilerParams(
            collective_id=0, has_side_effects=True, vmem_limit_bytes=48 * 1024 * 1024
        ),
    )(
        *[
            pltpu.with_memory_space_constraint(x, pltpu.HBM)
            for x in (widths, control, ensemble, source, weight, obs_mask, innovation)
        ]
    )


def solution(mesh):
    in_specs = (
        P("mem", "lat", None),
        P("mem", None, "lat", None),
        P("lat"),
        P(None, "lat", None),
        P(None, "lat", None),
        P(None, "lat", None),
        P(None, "lat", None),
    )
    out_specs = P("mem", "lat", None)
    return jax.shard_map(local, mesh=mesh, in_specs=in_specs, out_specs=out_specs, check_vma=False)
```
